32 devices in a mesh: slab: 4 (over z), energy: 8 (over y, x, core).
Axes of the slice: x: 2, y: 2, z: 4, core: 2. Of those that a mesh axis runs over, the one named last changes fastest.
Arguments:
- propagator: bfloat16 [2, 8, 8, 512, 512], P(None, 'slab', 'energy'), may hold values from -0.1875 to 0.1875
- source: bfloat16 [2, 8, 8, 512, 512], P(None, 'slab', 'energy'), may hold values from -4 to 4
- spectral: bfloat16 [2, 8, 8, 512, 512], P(None, 'slab', 'energy'), may hold values from -6 to 6
- coulomb: bfloat16 [8, 3, 512, 512], P('slab'), may hold values from -0.25 to 0.25
- v_pattern: int32 [8, 3], P('slab'), may hold values 0 or 1
Outputs:
- screened: bfloat16 [2, 8, 8, 512, 512], P(None, 'slab', 'energy')
The draws below stay inside these ranges and needn't reach their ends.
All inputs are finite; a program needn't handle non-finite values. No bound on the sum of `v_pattern` on one device may be relied on, other than what follows from the above.
Results may differ from the reference program's by a relative error of at most 0.038.
Values may be sent and summed in bfloat16 or wider, within the bound.
No kernel may reach another device: no remote copies, remote signals or barrier semaphores. Data moves between devices by JAX's collectives and lax.ppermute only.
A program may use at most 128 MiB of HBM per device.

```python
import jax
import jax.numpy as jnp
from jax import lax

B = 512
NSLAB = 8
NE = 8


def plant(values, stream_key, least, top_value):
    spot = [jax.random.randint(jax.random.fold_in(stream_key, axis), (), 0, length) for axis, length in enumerate(values.shape)]
    longest = values.shape.index(max(values.shape))
    beside = spot[:longest] + [(spot[longest] + 1) % values.shape[longest]] + spot[longest + 1:]
    return values.at[tuple(spot)].set(least).at[tuple(beside)].set(top_value)


def block_levels(rng, dims, pieces, low, high):
    loudness, own = 1.0, jax.random.fold_in(rng, 6)
    for dim, shards_of in pieces:
        steps = jnp.exp(jax.random.uniform(jax.random.fold_in(own, dim), (shards_of,), jnp.float32, low / len(pieces), high / len(pieces)))
        loudness = loudness * jnp.repeat(steps, dims[dim] // shards_of).reshape([-1 if axis == dim else 1 for axis in range(len(dims))])
    return loudness


def noise(key, dims, width, bound, shards=(), kind=jnp.bfloat16):
    level = block_levels(key, dims, shards, -0.22, 0.18) if shards else 1.0
    entries = jax.random.normal(key, dims, jnp.float32) * width * level
    return jnp.minimum(jnp.maximum(entries, -bound), bound).astype(kind)


def setup_inputs(seed: int = 0) -> dict:
    splits = jax.random.split(jax.random.key(seed), 6)
    return {
        "propagator": noise(splits[0], (2, NSLAB, NE, B, B), (2 * B) ** -0.5, 0.1875, ((1, 4), (2, 8))),
        "source": noise(splits[1], (2, NSLAB, NE, B, B), 0.5, 4.0, ((1, 4), (2, 8))),
        "spectral": noise(splits[2], (2, NSLAB, NE, B, B), 1.0, 6.0, ((1, 4), (2, 8))),
        "coulomb": noise(splits[3], (NSLAB, 3, B, B), B ** -0.5, 0.25, ((0, 4),)),
        "v_pattern": plant((jax.random.randint(splits[4], (NSLAB, 3), 0, 4) < 3).astype(jnp.int32), jax.random.fold_in(splits[4], 1), 0, 1),
    }


def complex_mul(left_op, right_op):
    def prod(one, two):
        return jnp.einsum('...ij,...jk->...ik', one, two)
    real_part = prod(left_op[0], right_op[0]) - prod(left_op[1], right_op[1])
    imag_part = prod(left_op[0], right_op[1]) + prod(left_op[1], right_op[0])
    return jnp.stack([real_part, imag_part])


def mul_adjoint(left_op, right_op):
    def prod(one, two):
        return jnp.einsum('...ij,...kj->...ik', one, two)
    real_part = prod(left_op[0], right_op[0]) + prod(left_op[1], right_op[1])
    imag_part = prod(left_op[1], right_op[0]) - prod(left_op[0], right_op[1])
    return jnp.stack([real_part, imag_part])


def sandwich(blocks, carried):
    rounded = lax.optimization_barrier(carried.astype(jnp.bfloat16)).astype(jnp.float32)
    inner = complex_mul(blocks, rounded)
    inner = lax.optimization_barrier(inner.astype(jnp.bfloat16)).astype(jnp.float32)
    return mul_adjoint(inner, blocks)


def reference(propagator, source, spectral, coulomb, v_pattern):
    carried = jnp.zeros((2, NE, B, B), jnp.float32)
    lesser_list = []
    for slab_idx in range(NSLAB):
        blocks = propagator[:, slab_idx].astype(jnp.float32)
        carried = sandwich(blocks, carried) + source[:, slab_idx].astype(jnp.float32)
        lesser_list.append(carried.astype(jnp.bfloat16))
    lesser = jnp.stack(lesser_list, axis=1)
    lesser_f = lesser.astype(jnp.float32)
    spectral_f = spectral.astype(jnp.float32)
    greater = jnp.stack([lesser_f[0] + spectral_f[1], lesser_f[1] - spectral_f[0]]).astype(jnp.bfloat16)
    padded_len = 2 * NE
    norm_scale = NE ** -0.5
    polar_list = []
    for slab_idx in range(NSLAB):
        lesser_c = lesser_f[0, slab_idx] + 1j * lesser_f[1, slab_idx]
        greater_f = jnp.swapaxes(greater[:, slab_idx].astype(jnp.float32), -1, -2)
        greater_t = greater_f[0] + 1j * greater_f[1]
        lesser_hat = jnp.fft.fft(lesser_c, n=padded_len, axis=0)
        greater_hat = padded_len * jnp.fft.ifft(greater_t, n=padded_len, axis=0)
        correlated = jnp.fft.ifft(lesser_hat * greater_hat, axis=0)[:NE]
        polar_list.append(jnp.stack([norm_scale * jnp.imag(correlated), -norm_scale * jnp.real(correlated)]).astype(jnp.bfloat16))
    polarization = jnp.stack(polar_list, axis=1)
    padded = jnp.pad(polarization, ((0, 0), (1, 1), (0, 0), (0, 0), (0, 0)))
    screened_list = []
    for slab_idx in range(NSLAB):
        summed = jnp.zeros((2, NE, B, B), jnp.float32)
        for offset_idx in range(3):
            coulomb_f = coulomb[slab_idx, offset_idx].astype(jnp.float32)
            polar_f = padded[:, slab_idx + offset_idx].astype(jnp.float32)
            inner_prod = jnp.einsum('ij,qejk->qeik', coulomb_f, polar_f)
            inner_prod = lax.optimization_barrier(inner_prod.astype(jnp.bfloat16)).astype(jnp.float32)
            outer_prod = jnp.einsum('qeik,lk->qeil', inner_prod, coulomb_f)
            summed = summed + v_pattern[slab_idx, offset_idx].astype(jnp.float32) * outer_prod
        screened_list.append(summed.astype(jnp.bfloat16))
    return jnp.stack(screened_list, axis=1)
```

```python
import functools

import jax
import jax.numpy as jnp
import numpy as np
from jax import lax
from jax.experimental import pallas as pl
from jax.experimental.pallas import tpu as pltpu
from jax.sharding import PartitionSpec as P


BF = jnp.bfloat16
F32 = jnp.float32
NN = (((1,), (0,)), ((), ()))
NT = (((1,), (1,)), ((), ()))


def tile_table(owners):
    side = round((2 * owners) ** 0.5)
    assert side * side == 2 * owners and side % 4 == 0
    half = side // 2
    even = [((p, q), (q, p)) for p in range(half) for q in range(p + 1, half)]
    odd = [((p, q), (q, p)) for p in range(half, side) for q in range(p + 1, side)]
    for p in range(half):
        for q in range(half, side):
            (even if (p + q) % 2 == 0 else odd).append(((p, q), (q, p)))
    diag = [((p, p), (p + half, p + half)) for p in range(half)]
    even += diag[0::2]
    odd += diag[1::2]
    assert len(even) == len(odd) == owners // 2
    table = np.zeros((owners, 2, 2), np.int32)
    table[0::2] = even
    table[1::2] = odd
    return side, table


def dot(a, b, dims):
    return lax.dot_general(a, b, dims, preferred_element_type=F32)


def call(kernel, outs, args, scratch=(), scalars=1):
    smem = pl.BlockSpec(memory_space=pltpu.SMEM)
    vmem = pl.BlockSpec(memory_space=pltpu.VMEM)
    args = list(args[:scalars]) + [
        pltpu.with_memory_space_constraint(x, pltpu.VMEM) for x in args[scalars:]
    ]
    return pl.pallas_call(
        kernel,
        out_shape=outs,
        in_specs=[smem] * scalars + [vmem] * (len(args) - scalars),
        out_specs=[vmem] * len(outs) if isinstance(outs, list) else vmem,
        scratch_shapes=list(scratch),
        compiler_params=pltpu.CompilerParams(vmem_limit_bytes=24 << 20),
    )(*args)


def struct(*shape, dtype=BF):
    return pltpu.VMEM(shape, dtype)


def rows_product(ar, ai, ah_r, ah_i, x, add_r, add_i):
    lhs = jnp.concatenate(
        [jnp.concatenate([ah_r, -ah_i], 1), jnp.concatenate([ah_i, ah_r], 1)], 0
    )
    inner = dot(lhs, x, NN).astype(BF)
    rows = ah_r.shape[0]
    inner_r, inner_i = inner[:rows], inner[rows:]
    lhs = jnp.concatenate(
        [jnp.concatenate([inner_r, inner_i], 1), jnp.concatenate([inner_i, -inner_r], 1)], 0
    )
    out = dot(lhs, jnp.concatenate([ar, ai], 1), NT)
    return (out[:rows] + add_r.astype(F32)).astype(BF), (out[rows:] + add_i.astype(F32)).astype(BF)


def first_rows(pos, flip, propagator, source):
    size = propagator.shape[-1]
    half = size // 2

    def kernel(pos, a, s, out):
        at = pl.multiple_of((pos[0] ^ flip) * half, half)
        rows = pl.ds(at, half)
        x = jnp.concatenate([s[0, 0], s[1, 0]], 0)
        out[0], out[1] = rows_product(
            a[0, 1], a[1, 1], a[0, 1, rows], a[1, 1, rows], x, s[0, 1, rows], s[1, 1, rows]
        )

    return call(kernel, struct(2, half, size), (pos, propagator, source))


def next_rows(pos, blocks, slab, mine, other, add, add_slab):
    size = blocks.shape[-1]
    half = size // 2

    def kernel(pos, a, m, o, s, out, xs):
        c = pos[0]
        rows = pl.ds(pl.multiple_of(c * half, half), half)
        for r in range(2):
            xs[pl.ds(pl.multiple_of(r * size + c * half, half), half)] = m[r]
            xs[pl.ds(pl.multiple_of(r * size + (1 - c) * half, half), half)] = o[r]
        if slab is None:
            ar, ai, hr, hi = a[0], a[1], a[0, rows], a[1, rows]
            sr, si = s[0], s[1]
        else:
            ar, ai, hr, hi = a[0, slab], a[1, slab], a[0, slab, rows], a[1, slab, rows]
            sr, si = s[0, add_slab, rows], s[1, add_slab, rows]
        out[0], out[1] = rows_product(ar, ai, hr, hi, xs[...], sr, si)

    return call(
        kernel,
        struct(2, half, size),
        (pos, blocks, mine, other, add),
        [pltpu.VMEM((2 * size, size), BF)],
    )


def total_map(pos, blocks):
    size = blocks.shape[-1]

    def kernel(pos, a, out):
        lhs = jnp.concatenate(
            [
                jnp.concatenate([a[0, 1], -a[1, 1]], 1),
                jnp.concatenate([a[1, 1], a[0, 1]], 1),
            ],
            0,
        )
        res = dot(lhs, jnp.concatenate([a[0, 0], a[1, 0]], 0), NN).astype(BF)
        out[0] = res[:size]
        out[1] = res[size:]

    return call(kernel, struct(2, size, size), (pos, blocks))


def pack_tiles(pos, table, side, mine, other, chips):
    size = mine.shape[-1]
    half = size // 2
    tile = size // side

    def kernel(pos, tab, m, o, *rest):
        outs, ls = rest[:-1], rest[-1]
        c, h = pos[0], pos[1]
        for r in range(2):
            for q in range(side):
                ls[r, q, pl.ds(pl.multiple_of(c * half, half), half)] = m[r, :, q * tile : (q + 1) * tile]
                ls[r, q, pl.ds(pl.multiple_of((1 - c) * half, half), half)] = o[r, :, q * tile : (q + 1) * tile]
        for d in range(chips):
            owner = 2 * (h ^ d) + c
            for t in range(2):
                p, q = tab[owner * 4 + t * 2], tab[owner * 4 + t * 2 + 1]
                at = pl.ds(pl.multiple_of(p * tile, tile), tile)
                for r in range(2):
                    outs[d][r, t] = ls[r, q, at]

    return call(
        kernel,
        [struct(2, 2, tile, tile)] * chips,
        (pos, table, mine, other),
        [pltpu.VMEM((2, side, size, tile), BF)],
        scalars=2,
    )


def pack_spectral(pos, table, side, spectral, chips):
    slabs, size = spectral.shape[1], spectral.shape[-1]
    tile = size // side

    def kernel(pos, tab, sp, keep, send, ls):
        c, h = pos[0], pos[1]
        for s in range(slabs):
            for r in range(2):
                for q in range(side):
                    ls[r, q] = sp[r, s, :, q * tile : (q + 1) * tile]
            for flip, out in ((0, keep), (1, send)):
                for d in range(chips):
                    owner = 2 * (h ^ d) + (c ^ flip)
                    for t in range(2):
                        p, q = tab[owner * 4 + t * 2], tab[owner * 4 + t * 2 + 1]
                        at = pl.ds(pl.multiple_of(p * tile, tile), tile)
                        for r in range(2):
                            out[d, s, r, t] = ls[r, q, at]

    shape = struct(chips, slabs, 2, 2, tile, tile)
    return call(
        kernel,
        [shape, shape],
        (pos, table, spectral),
        [pltpu.VMEM((2, side, size, tile), BF)],
        scalars=2,
    )


def correlate(pos, table, slab, first, second, own, partner):
    chips = len(first)
    count = 2 * chips
    tile = first[0].shape[-1]
    scale = count**-0.5

    def kernel(pos, tab, *rest):
        ls = (rest[:chips], rest[chips : 2 * chips])
        sps = (rest[2 * chips : 3 * chips], rest[3 * chips : 4 * chips])
        outs = rest[4 * chips : 4 * chips + count]
        lf, gt, pf = rest[4 * chips + count :]
        c, h, i = pos[0], pos[1], pos[2]
        off = jnp.where(tab[i * 4] == tab[i * 4 + 1], 0, 1)
        eye = (
            lax.broadcasted_iota(jnp.int32, (tile, tile), 0)
            == lax.broadcasted_iota(jnp.int32, (tile, tile), 1)
        ).astype(F32).astype(BF)

        def fill(e, sp):
            for d in range(chips):
                m = 2 * (h ^ d) + e
                for t in range(2):
                    lr = ls[0][d][0, t].astype(F32) if e == 0 else ls[1][d][0, t].astype(F32)
                    li = ls[0][d][1, t].astype(F32) if e == 0 else ls[1][d][1, t].astype(F32)
                    lf[m, 0, t] = lr
                    lf[m, 1, t] = li
                    gr = (lr + sp[d][slab, 1, t].astype(F32)).astype(BF)
                    gi = (li - sp[d][slab, 0, t].astype(F32)).astype(BF)
                    gt[m, 0, t ^ off] = dot(eye, gr, NT)
                    gt[m, 1, t ^ off] = dot(eye, gi, NT)

        @pl.when(c == 0)
        def _():
            fill(0, sps[0])
            fill(1, sps[1])

        @pl.when(c == 1)
        def _():
            fill(0, sps[1])
            fill(1, sps[0])

        steps = tile // 8

        def chunk(step, _):
            t = step // steps
            rows = pl.ds(pl.multiple_of((step % steps) * 8, 8), 8)
            if count <= 8:
                lr = [lf[m, 0, t, rows] for m in range(count)]
                li = [lf[m, 1, t, rows] for m in range(count)]
                gr = [gt[m, 0, t, rows] for m in range(count)]
                gi = [gt[m, 1, t, rows] for m in range(count)]
                for k in range(count):
                    re = sum(lr[m] * gr[m - k] - li[m] * gi[m - k] for m in range(k, count))
                    im = sum(lr[m] * gi[m - k] + li[m] * gr[m - k] for m in range(k, count))
                    pf[k, 0, t, rows] = scale * im
                    pf[k, 1, t, rows] = -scale * re
            else:

                def lag(k, _):
                    def term(m, acc):
                        re, im = acc
                        lr, li = lf[m, 0, t, rows], lf[m, 1, t, rows]
                        gr, gi = gt[m - k, 0, t, rows], gt[m - k, 1, t, rows]
                        return re + (lr * gr - li * gi), im + (lr * gi + li * gr)

                    zero = jnp.zeros((8, tile), F32)
                    re, im = lax.fori_loop(k, count, term, (zero, zero))
                    pf[k, 0, t, rows] = scale * im
                    pf[k, 1, t, rows] = -scale * re
                    return 0

                lax.fori_loop(0, count, lag, 0)
            return 0

        lax.fori_loop(0, 2 * steps, chunk, 0)
        for d in range(count):
            outs[d][...] = pf[i ^ d].astype(BF)

    big = pltpu.VMEM((count, 2, 2, tile, tile), F32)
    return call(
        kernel,
        [struct(2, 2, tile, tile)] * count,
        (pos, table, *first, *second, *own, *partner),
        [big, big, big],
        scalars=2,
    )


def assemble(tab, i, side, tile, offsets, groups, dest):
    for group, ds in zip(groups, offsets):
        for g, d in enumerate(ds):
            owner = i ^ d
            for t in range(2):
                p, q = tab[owner * 4 + t * 2], tab[owner * 4 + t * 2 + 1]
                at = pl.ds(pl.multiple_of(p * tile, tile), tile)
                for r in range(2):
                    dest[r, q, at] = group[g, r, t]


def coulomb_pair(block, p, side):
    size = block.shape[-1]
    cols = jnp.concatenate([p[r, q] for r in range(2) for q in range(side)], 1)
    left = dot(block, cols, NN).astype(BF)
    return dot(jnp.concatenate([left[:, :size], left[:, size:]], 0), block, NT)


def screen_own(pos, table, pattern, side, offsets, coulomb, groups):
    slabs, size = coulomb.shape[0], coulomb.shape[-1]
    tile = size // side
    ng = len(offsets)

    def kernel(pos, tab, v, cb, *rest):
        ins, out, p = rest[: slabs * ng], rest[slabs * ng], rest[slabs * ng + 1]
        i = pos[2]
        out[...] = jnp.zeros_like(out)
        for s in range(slabs):
            assemble(tab, i, side, tile, offsets, ins[s * ng : (s + 1) * ng], p.at[s])
        for s in range(slabs):
            for a in range(3):
                src = s + a - 1
                if 0 <= src < slabs:

                    @pl.when(v[s, a] != 0)
                    def _():
                        weight = v[s, a].astype(F32)
                        out[s] += weight * coulomb_pair(cb[s, a], p.at[src], side)

    return call(
        kernel,
        struct(slabs, 2 * size, size, dtype=F32),
        (pos, table, pattern, coulomb, *[g for s in groups for g in s]),
        [pltpu.VMEM((slabs, 2, side, size, tile), BF)],
        scalars=3,
    )


def screen_edges(pos, table, pattern, side, offsets, coulomb, total, low, high):
    slabs, size = coulomb.shape[0], coulomb.shape[-1]
    tile = size // side
    ng = len(offsets)

    def kernel(pos, tab, v, cb, tot, *rest):
        ins, out, p = rest[: 2 * ng], rest[2 * ng], rest[2 * ng + 1]
        i = pos[2]
        acc = rest[2 * ng + 2]
        for e, (s, a) in enumerate(((0, 0), (slabs - 1, 2))):
            acc[e] = tot[s]

            @pl.when(v[s, a] != 0)
            def _():
                assemble(tab, i, side, tile, offsets, ins[e * ng : (e + 1) * ng], p)
                acc[e] += v[s, a].astype(F32) * coulomb_pair(cb[s, a], p, side)

        for s in range(slabs):
            for r in range(2):
                rows = slice(r * size, (r + 1) * size)
                if s == 0:
                    res = acc[0, rows]
                elif s == slabs - 1:
                    res = acc[1, rows]
                else:
                    res = tot[s, rows]
                out[r, s] = res.astype(BF)

    return call(
        kernel,
        struct(2, slabs, size, size),
        (pos, table, pattern, coulomb, total, *low, *high),
        [pltpu.VMEM((2, side, size, tile), BF), pltpu.VMEM((2, 2 * size, size), F32)],
        scalars=3,
    )


def body(propagator, source, spectral, coulomb, v_pattern):
    slabs, size = propagator.shape[1], propagator.shape[-1]
    assert slabs == 2
    count = lax.axis_size("energy")
    chips = count // 2
    zs = lax.axis_size("slab")
    side, table = tile_table(count)
    table = jnp.asarray(table.reshape(-1))
    i = lax.axis_index("energy").astype(jnp.int32)
    c = i % 2
    pos = jnp.stack([c, i // 2, i])
    flat = (2, slabs, size, size)
    prop, src, spec = propagator.reshape(flat), source.reshape(flat), spectral.reshape(flat)

    def partner(x):
        return lax.ppermute(x, "energy", [(j, j ^ 1) for j in range(count)])

    def chip(x, d):
        return lax.ppermute(x, "energy", [(j, j ^ (2 * d)) for j in range(count)])

    def device(x, d):
        return lax.ppermute(x, "energy", [(j, j ^ d) for j in range(count)])

    even = c == 0

    def by_energy(own, other):
        return jnp.where(even, own, other), jnp.where(even, other, own)

    send = first_rows(pos, 1, prop, src)
    got = partner(send)
    keep = first_rows(pos, 0, prop, src)
    offset = by_energy(keep, got)
    outgoing = offset
    prop_e = by_energy(prop, partner(prop))
    src_e = by_energy(src, partner(src))
    maps = [total_map(pos, b) for b in prop_e]
    sp_keep, sp_send = pack_spectral(pos, table, side, spec, chips)
    sp_got = partner(sp_send)
    sp_own = [sp_keep[0]] + [chip(sp_keep[d], d) for d in range(1, chips)]
    sp_part = [sp_got[0]] + [chip(sp_got[d], d) for d in range(1, chips)]

    incoming = [jnp.zeros_like(o) for o in offset]
    for turn in range(zs - 1):
        pairs = [(z, z + 1) for z in range(min(turn + 1, zs - 1))]
        incoming = [lax.ppermute(o, "slab", pairs) for o in outgoing]
        if turn < zs - 2:
            outgoing = [
                next_rows(pos, maps[e], None, incoming[e], partner(incoming[e]), offset[e], None)
                for e in range(2)
            ]
    packed = []
    carried = incoming
    for e in range(2):
        mine = incoming[e]
        per_slab = []
        for s in range(slabs):
            mine = next_rows(pos, prop_e[e], s, mine, partner(mine), src_e[e], s)
            tiles = pack_tiles(pos, table, side, mine, partner(mine), chips)
            per_slab.append([tiles[0]] + [chip(tiles[d], d) for d in range(1, chips)])
        packed.append(per_slab)
    offsets = ([d for d in range(count) if d < count // 2], [d for d in range(count) if d >= count // 2])
    groups = []
    for s in range(slabs):
        tiles = correlate(pos, table, s, packed[0][s], packed[1][s], sp_own, sp_part)
        back = [tiles[0]] + [device(tiles[d], d) for d in range(1, count)]
        groups.append([jnp.stack([back[d] for d in ds]) for ds in offsets])
    up = [(z, z + 1) for z in range(zs - 1)]
    down = [(z + 1, z) for z in range(zs - 1)]
    high = [lax.ppermute(g, "slab", down) for g in groups[0]]
    low = [lax.ppermute(g, "slab", up) for g in groups[slabs - 1]]
    total = screen_own(pos, table, v_pattern, side, offsets, coulomb, groups)
    out = screen_edges(pos, table, v_pattern, side, offsets, coulomb, total, low, high)
    return out[:, :, None]


def solution(mesh):
    placed = (
        P(None, "slab", "energy", None, None),
        P(None, "slab", "energy", None, None),
        P(None, "slab", "energy", None, None),
        P("slab", None, None, None),
        P("slab", None),
    )
    return jax.shard_map(
        body,
        mesh=mesh,
        in_specs=placed,
        out_specs=P(None, "slab", "energy", None, None),
        check_vma=False,
    )
```
